256 devices in a mesh: rep: 8 (over z_lo, x), exp: 32 (over y, z_hi, core).
Axes of the slice: x: 4, y: 4, z: 8 (z_hi: 4, z_lo: 2; z = z_hi * 2 + z_lo), core: 2. Of those that a mesh axis runs over, the one named last changes fastest.
Arguments:
- hidden: bfloat16 [4096, 7168], P(('rep', 'exp')), may hold values from -6 to 6
- expert_ids: int32 [4096, 8], P(('rep', 'exp')), may hold values from 0 to 15, all different within a row; in each aligned block of 16 rows (0 to 15, 16 to 31, ...) at most 10 rows name the same one
- router: bfloat16 [7168, 16], replicated, may hold values from -0.0625 to 0.0625
- gate_up: bfloat16 [32, 512, 2, 7168], P('exp', 'rep'), may hold values from -0.0625 to 0.0625
- down_weight: bfloat16 [32, 512, 7168], P('exp', 'rep'), may hold values from -0.1875 to 0.1875
- query_latent: bfloat16 [4096, 64, 512], P(('rep', 'exp')), may hold values from -110 to 110
- query_rope: bfloat16 [4096, 64, 64], P(('rep', 'exp')), may hold values from -6 to 6
- cache_latent: bfloat16 [4096, 256, 512], P(('rep', 'exp')), may hold values from -8 to 8
- cache_rope: bfloat16 [4096, 64, 256], P(('rep', 'exp')), may hold values from -5 to 5
- lengths: int32 [4096], P(('rep', 'exp')), may hold values from 32 to 256, as said below
Outputs:
- moe_out: bfloat16 [4096, 7168], P(('rep', 'exp'))
- attn_latent: bfloat16 [4096, 64, 512], P(('rep', 'exp'))
The draws below stay inside these ranges and needn't reach their ends.
Inputs may be any that keep to these rules, and one draw needn't show every extreme that they name: `expert_ids`: in every aligned block of 16 rows no expert is named by more than 10 pairs, a bound that some block reaches. `lengths`: some row has length 256.
All inputs are finite; a program needn't handle non-finite values.
Results may differ from the reference program's by a relative error of at most 0.015.
Values may be sent and summed in bfloat16 or wider, within the bound.
No kernel may reach another device: no remote copies, remote signals or barrier semaphores. Data moves between devices by JAX's collectives and lax.ppermute only.
A program may use at most 128 MiB of HBM per device.

```python
import math
from functools import partial
import jax
import jax.numpy as jnp
import numpy as np
from jax import lax

D = 7168
EXPERT_HIDDEN = 1024
NH = 64
KVL = 512
ROPE = 64
NOPE = 128
TOP = 8
ROWS = 16
LEN = 256
HID_DEV = 512
EXPERTS = 16
CAP = 10
TOKENS = 4096
N_REP = 8
N_EXP = 32


def pair_keys(key):
    first_keys = jax.random.truncated_normal(jax.random.fold_in(key, 21), -5.0, 5.0, (TOKENS, 2, KVL), jnp.float32)
    rope_keys = jax.random.truncated_normal(jax.random.fold_in(key, 22), -5.0, 5.0, (TOKENS, ROPE, 2), jnp.float32)
    return (first_keys, rope_keys)


def draw_cache_latent(key, part):
    first_keys, rope_keys = pair_keys(key)
    remaining = jax.random.truncated_normal(jax.random.fold_in(key, 23), -5.0, 5.0, (TOKENS, LEN - 2, KVL), jnp.float32)
    return jnp.concatenate((first_keys, remaining), axis=1).astype(jnp.bfloat16)


def draw_cache_rope(key, part):
    first_keys, rope_keys = pair_keys(key)
    remaining = jax.random.truncated_normal(jax.random.fold_in(key, 24), -5.0, 5.0, (TOKENS, ROPE, LEN - 2), jnp.float32)
    return jnp.concatenate((rope_keys, remaining), axis=2).astype(jnp.bfloat16)


def draw_query_latent(key, part):
    base_draw = jax.random.truncated_normal(jax.random.fold_in(key, 25), -5.0, 5.0, (TOKENS, NH, KVL), jnp.float32)
    return base_draw.astype(jnp.bfloat16)


def draw_query_rope(key, part):
    base_draw = jax.random.truncated_normal(jax.random.fold_in(key, 26), -5.0, 5.0, (TOKENS, NH, ROPE), jnp.float32)
    return base_draw.astype(jnp.bfloat16)


def draw_lengths(key, part):
    drawn = jax.random.randint(jax.random.fold_in(key, 31), (TOKENS,), max(2, LEN // 8), LEN + 1, dtype=jnp.int32)
    return jnp.where(jnp.arange(TOKENS, dtype=jnp.int32) == 0, LEN, drawn).astype(jnp.int32)


def block_scale(stream_key, shape, shards, low, top_value):
    gain, own = 1.0, jax.random.fold_in(stream_key, 6)
    for axis_at, shards_of in shards:
        draws = jnp.exp(jax.random.uniform(jax.random.fold_in(own, axis_at), (shards_of,), jnp.float32, low / len(shards), top_value / len(shards)))
        gain = gain * jnp.repeat(draws, shape[axis_at] // shards_of).reshape([-1 if axis == axis_at else 1 for axis in range(len(shape))])
    return gain


def deal_out(stream_key, own, number, rows, amount, top, limit, skew):
    sequence = jax.random.permutation(stream_key, amount)
    crowded, common = load_shares(amount, rows * top, limit, skew, True), load_shares(amount, rows * top, limit, skew, False)
    places = jnp.arange(amount)

    def named(sizes, offset_by):
        used = int((sizes > 0).sum())
        fixed = max(1, used // 4)
        passed = fixed + (places - fixed + offset_by * (used - fixed)) % max(1, amount - fixed)
        return jnp.zeros((amount,), jnp.int32).at[sequence[jnp.where(places < fixed, places, passed)]].set(jnp.asarray(sizes, jnp.int32))

    sizes = jnp.where(number % 4 == 0, named(crowded, number // 4), named(common, number - number // 4 - 1))
    mixed = jax.random.permutation(jax.random.fold_in(own, 3), amount)
    giver, sink = mixed[0:amount // 2 * 2:2], mixed[1:amount // 2 * 2:2]
    slack = jnp.minimum(sizes[giver] - 1, limit - sizes[sink]) // 2
    slack = jnp.where((giver == sequence[0]) | (sink == sequence[0]) | (sizes[sink] == 0), 0, jnp.maximum(slack, 0))
    passed = jax.random.randint(jax.random.fold_in(own, 4), (amount // 2,), 0, 1 << 20) % (slack + 1)
    sizes = sizes.at[giver].add(-passed).at[sink].add(passed)
    labels = jnp.searchsorted(jnp.cumsum(sizes), jnp.arange(rows * top), side="right").astype(jnp.int32)
    listing = labels.reshape(top, rows).T
    listing = listing[jax.random.permutation(jax.random.fold_in(own, 1), rows)]
    offset_by = jax.random.randint(jax.random.fold_in(own, 2), (rows, 1), 0, top)
    return jnp.take_along_axis(listing, (jnp.arange(top)[None, :] + offset_by) % top, axis=1)


def load_shares(amount, total, limit, lean, full):
    portions = [(1 << 20) // math.isqrt(rank ** lean) + 1 for rank in range(1, amount + 1)]
    largest = limit if full else min(limit, max(-(-total // amount), total * portions[0] // sum(portions)))
    least = 1 if total - largest >= amount - 1 else 0
    holding, surplus = [largest] + [least] * (amount - 1), total - largest - least * (amount - 1)
    while surplus > 0:
        movable = [i for i in range(1, amount) if holding[i] < largest] or [i for i in range(1, amount) if holding[i] < limit]
        whole, left = sum([portions[i] for i in movable]), surplus
        for i in movable:
            extra = min(limit - holding[i], max(1, left * portions[i] // whole), surplus)
            holding[i] = holding[i] + extra
            surplus = surplus - extra
    return np.array(holding)


def gaussian(own_key, extent, deviation, limit, split=(), kind=jnp.bfloat16):
    gain = block_scale(own_key, extent, split, -0.22, 0.18) if split else 1.0
    values = jax.random.normal(own_key, extent, jnp.float32) * deviation * gain
    return jnp.minimum(jnp.maximum(values, -limit), limit).astype(kind)


def setup_inputs(seed: int = 0) -> dict:
    streams_of = jax.random.split(jax.random.key(seed), 11)
    hidden = gaussian(streams_of[0], (TOKENS, D), 1.0, 6.0, ((0, 256),))
    expert_ids_keys = jax.random.split(jax.random.fold_in(streams_of[1], 1), TOKENS // ROWS)
    expert_ids_turns = jax.random.permutation(jax.random.fold_in(streams_of[1], 3), TOKENS // ROWS)
    expert_ids = jax.vmap(lambda own, number: deal_out(jax.random.fold_in(streams_of[1], 2), own, number, ROWS, EXPERTS, TOP, CAP, 2))(expert_ids_keys, expert_ids_turns).reshape((TOKENS, TOP))
    router = gaussian(streams_of[2], (D, EXPERTS), D ** -0.5, 0.0625)
    gate_up = gaussian(streams_of[3], (N_EXP, HID_DEV, 2, D), D ** -0.5, 0.0625, ((0, 32), (1, 8)))
    down_weight = gaussian(streams_of[4], (N_EXP, HID_DEV, D), EXPERT_HIDDEN ** -0.5, 0.1875, ((0, 32), (1, 8)))
    query_latent = draw_query_latent(jax.random.fold_in(streams_of[10], 71), 0)
    query_rope = draw_query_rope(jax.random.fold_in(streams_of[10], 71), 0)
    cache_latent = draw_cache_latent(jax.random.fold_in(streams_of[10], 71), 0)
    cache_rope = draw_cache_rope(jax.random.fold_in(streams_of[10], 71), 0)
    lengths = draw_lengths(jax.random.fold_in(streams_of[10], 71), 0)
    return dict(hidden=hidden, expert_ids=expert_ids, router=router, gate_up=gate_up, down_weight=down_weight, query_latent=query_latent, query_rope=query_rope, cache_latent=cache_latent, cache_rope=cache_rope, lengths=lengths)


route_scale = 2.827

def slot_table(expert_ids, experts, capacity):
    flat_ids = expert_ids.reshape(-1).astype(jnp.int32)
    onehot = (flat_ids[:, None] == jnp.arange(experts, dtype=jnp.int32)[None, :]).astype(jnp.int32)
    earlier = (jnp.cumsum(onehot, axis=0) - onehot).astype(jnp.int32)
    slot_rank = lax.optimization_barrier(jnp.sum(earlier * onehot, axis=1)).astype(jnp.int32)
    return (flat_ids * capacity + slot_rank).astype(jnp.int32)

def bucket_rows(rows_in, flat_slot, experts, capacity):
    row_total = rows_in.shape[0]
    pair_total = flat_slot.shape[0]
    slot_matrix = (jnp.arange(experts * capacity, dtype=jnp.int32)[:, None] == flat_slot[None, :]).astype(jnp.float32)
    slot_matrix = lax.optimization_barrier(jnp.sum(slot_matrix.reshape(experts * capacity, row_total, pair_total // row_total), axis=2))
    return jnp.dot(slot_matrix.astype(jnp.bfloat16), rows_in, preferred_element_type=jnp.float32).astype(jnp.bfloat16)

def partial_output(rows_in, gate_up, down_weight):
    dims = (((1,), (1,)), ((), ()))
    gate_value = lax.dot_general(rows_in, gate_up[:, 0, :], dims, preferred_element_type=jnp.float32)
    up_value = lax.dot_general(rows_in, gate_up[:, 1, :], dims, preferred_element_type=jnp.float32)
    activated = (jax.nn.silu(gate_value) * up_value).astype(jnp.bfloat16)
    return jnp.dot(activated, down_weight, preferred_element_type=jnp.float32)

def attend(query_latent, query_rope, cache_latent, cache_rope, row_lengths):
    score_scale = 1.0 / math.sqrt(NOPE + ROPE)
    scores = jnp.einsum('rhc,rlc->rhl', query_latent.astype(jnp.float32), cache_latent.astype(jnp.float32))
    scores = scores + jnp.einsum('rhp,rpl->rhl', query_rope.astype(jnp.float32), cache_rope.astype(jnp.float32))
    scores = scores * score_scale
    valid_mask = jnp.arange(cache_latent.shape[1], dtype=jnp.int32)[None, None, :] < row_lengths[:, None, None]
    scores = jnp.where(valid_mask, scores, -1e+30)
    row_max = lax.optimization_barrier(jnp.max(scores, axis=2, keepdims=True))
    weights_raw = jnp.where(valid_mask, jnp.exp(scores - row_max), 0.0)
    attn_probs = (weights_raw / lax.optimization_barrier(jnp.sum(weights_raw, axis=2, keepdims=True))).astype(jnp.bfloat16)
    output = jnp.einsum('rhl,rlc->rhc', attn_probs.astype(jnp.float32), cache_latent.astype(jnp.float32))
    return output.astype(jnp.bfloat16)

def pick_rows(slot_matrix, row_index):
    return jnp.take(slot_matrix, row_index, axis=0)

def reference(hidden, expert_ids, router, gate_up, down_weight, query_latent, query_rope, cache_latent, cache_rope, lengths):
    devices = N_REP * N_EXP
    logits = jnp.dot(hidden, router, preferred_element_type=jnp.float32)
    picked = jnp.take_along_axis(logits, expert_ids, axis=1)
    sigmoid_scores = jax.nn.sigmoid(picked)
    mixing = sigmoid_scores / lax.optimization_barrier(jnp.sum(sigmoid_scores, axis=1, keepdims=True)) * route_scale
    id_blocks = expert_ids.reshape(devices, ROWS * TOP)
    slot_blocks = jax.vmap(partial(slot_table, experts=EXPERTS, capacity=CAP))(id_blocks)
    hidden_blocks = hidden.reshape(devices, ROWS, D)
    buckets = jax.vmap(partial(bucket_rows, experts=EXPERTS, capacity=CAP))(hidden_blocks, slot_blocks)
    buckets = buckets.reshape(devices, EXPERTS, CAP, D).transpose(1, 0, 2, 3).reshape(EXPERTS, devices * CAP, D)
    pair_gate_up = gate_up.reshape(EXPERTS, 2, HID_DEV, 2, D)
    pair_down = down_weight.reshape(EXPERTS, 2, HID_DEV, D)

    def one_expert(member_items):
        rows_in, expert_gate_up, expert_down = member_items
        front_part = partial_output(rows_in, expert_gate_up[0], expert_down[0]).astype(jnp.bfloat16)
        back_part = partial_output(rows_in, expert_gate_up[1], expert_down[1]).astype(jnp.bfloat16)
        return (front_part.astype(jnp.float32) + back_part.astype(jnp.float32)).astype(jnp.bfloat16)
    results = lax.map(one_expert, (buckets, pair_gate_up, pair_down))
    results = results.reshape(EXPERTS, devices, CAP, D).transpose(1, 0, 2, 3).reshape(devices, EXPERTS * CAP, D)
    chosen = jax.vmap(pick_rows)(results, slot_blocks).reshape(hidden.shape[0], TOP, D)
    moe_out = lax.optimization_barrier(jnp.sum(chosen.astype(jnp.float32) * mixing[:, :, None], axis=1)).astype(jnp.bfloat16)

    def attend_block(member_items):
        return attend(*member_items)
    attn_latent = lax.map(attend_block, (query_latent.reshape(devices, ROWS, NH, KVL), query_rope.reshape(devices, ROWS, NH, ROPE), cache_latent.reshape(devices, ROWS, LEN, KVL), cache_rope.reshape(devices, ROWS, ROPE, LEN), lengths.reshape(devices, ROWS))).reshape(hidden.shape[0], NH, KVL)
    return (moe_out, attn_latent)
```

```python
import math

import jax
import jax.numpy as jnp
from jax import lax
from jax.sharding import PartitionSpec as P

ROPE = 64
NOPE = 128
ROUTE_SCALE = 2.827
NX, NY, NZH, NZL, NC = 4, 4, 4, 2, 2
NZ = NZH * NZL
AXES = ("rep", "exp")


def index_of(x, y, z, c):
    return (((z % 2) * NX + x) * NY + y) * NZH * NC + (z // 2) * NC + c


def shift(value, x=0, y=0, z=0, c=0):
    pairs = []
    for i in range(NX):
        for j in range(NY):
            for k in range(NZ):
                for m in range(NC):
                    pairs.append(
                        (
                            index_of(i, j, k, m),
                            index_of((i + x) % NX, (j + y) % NY, (k + z) % NZ, (m + c) % NC),
                        )
                    )
    return lax.ppermute(value, AXES, pairs)


def gather_z(block):
    half = block.shape[1] // 256 * 128
    got = {0: block}
    up, down = block, block
    for step in range(1, NZ // 2):
        up, down = shift(up, z=1), shift(down, z=-1)
        got[NZ - step], got[step] = up, down
    far = (shift(up[:, :half], z=1), shift(down[:, half:], z=-1))
    got[NZ // 2] = jnp.concatenate(far, axis=1)
    return [got[d] for d in range(NZ)]


def gather_y(block):
    return [block] + [shift(block, y=-d) for d in range(1, NY)]


def scatter_y(blocks):
    total = blocks[0].astype(jnp.float32)
    for d in range(1, NY):
        total = total + shift(blocks[d], y=d).astype(jnp.float32)
    return total.astype(jnp.bfloat16)


def add(a, b):
    return (a.astype(jnp.float32) + b.astype(jnp.float32)).astype(jnp.bfloat16)


def scatter_z(blocks):
    half = blocks[0].shape[1] // 256 * 128
    far = NZ // 2
    up = shift(blocks[far][:, :half], z=1)
    down = shift(blocks[far][:, half:], z=-1)
    near = blocks[far - 1]
    up = jnp.concatenate([add(up, near[:, :half]), near[:, half:]], axis=1)
    near = blocks[far + 1]
    down = jnp.concatenate([near[:, :half], add(down, near[:, half:])], axis=1)
    for step in range(far - 1, 0, -1):
        up, down = shift(up, z=1), shift(down, z=-1)
        if step > 1:
            up, down = add(up, blocks[step - 1]), add(down, blocks[NZ - step + 1])
    return (
        blocks[0].astype(jnp.float32) + up.astype(jnp.float32) + down.astype(jnp.float32)
    ).astype(jnp.bfloat16)


def gather_x(first, second):
    first_left, first_right = shift(first, x=1), shift(first, x=-1)
    second_left, second_right = shift(second, x=1), shift(second, x=-1)
    first_far, second_far = shift(first_left, x=1), shift(second_right, x=-1)
    return (
        [first, first_left, first_right, first_far],
        [second, second_left, second_right, second_far],
    )


def attend(query_latent, query_rope, cache_latent, cache_rope, row_lengths):
    score_scale = 1.0 / math.sqrt(NOPE + ROPE)
    scores = jnp.einsum(
        "rhc,rlc->rhl", query_latent, cache_latent, preferred_element_type=jnp.float32
    )
    scores = scores + jnp.einsum(
        "rhp,rpl->rhl", query_rope, cache_rope, preferred_element_type=jnp.float32
    )
    scores = scores * score_scale
    valid_mask = (
        jnp.arange(cache_latent.shape[1], dtype=jnp.int32)[None, None, :]
        < row_lengths[:, None, None]
    )
    scores = jnp.where(valid_mask, scores, -1e30)
    row_max = jnp.max(scores, axis=2, keepdims=True)
    weights_raw = jnp.where(valid_mask, jnp.exp(scores - row_max), 0.0)
    attn_probs = (weights_raw / jnp.sum(weights_raw, axis=2, keepdims=True)).astype(jnp.bfloat16)
    output = jnp.einsum(
        "rhl,rlc->rhc", attn_probs, cache_latent, preferred_element_type=jnp.float32
    )
    return output.astype(jnp.bfloat16)


def mixing_table(hidden, expert_ids, router):
    logits = jnp.dot(hidden, router, preferred_element_type=jnp.float32)
    experts = router.shape[1]
    named = jnp.any(
        expert_ids[:, :, None] == jnp.arange(experts, dtype=jnp.int32)[None, None, :], axis=1
    )
    gates = jnp.where(named, jax.nn.sigmoid(logits), 0.0)
    return gates / jnp.sum(gates, axis=1, keepdims=True) * ROUTE_SCALE


def on_device(
    hidden,
    expert_ids,
    router,
    gate_up,
    down_weight,
    query_latent,
    query_rope,
    cache_latent,
    cache_rope,
    lengths,
):
    rows, width = hidden.shape
    units = gate_up.shape[1]
    experts = router.shape[1]
    cut = width // 2

    own_weights = gate_up[0].transpose(1, 0, 2).reshape(2 * units, width)
    weights_a, weights_b = gather_x(own_weights[:, :cut], own_weights[:, cut:])

    mixing = mixing_table(hidden, expert_ids, router)
    high = lax.reduce_precision(mixing, 8, 7)
    low = mixing - high
    table = jnp.concatenate([high, low], axis=1).astype(jnp.bfloat16)
    table = jnp.pad(table, ((0, 0), (0, 128 - 2 * experts)))
    part_a = hidden[:, :cut]
    part_b = jnp.concatenate([hidden[:, cut:], table], axis=1)

    rows_a = gather_y(jnp.concatenate(gather_z(part_a), axis=0))
    rows_b = gather_z(jnp.concatenate(gather_y(part_b), axis=0))
    twin_a = [shift(v, c=1) for v in rows_a]
    twin_b = [shift(v, c=1) for v in rows_b]
    all_a = jnp.concatenate(rows_a + twin_a, axis=0)
    all_b = jnp.concatenate(rows_b + twin_b, axis=0)
    count = all_a.shape[0]
    all_b = (
        all_b.reshape(NC, NZ, NY, rows, -1).transpose(0, 2, 1, 3, 4).reshape(count, all_b.shape[1])
    )

    dims = (((1,), (1,)), ((), ()))
    full_a = jnp.concatenate(weights_a, axis=0)
    full_b = jnp.concatenate(weights_b, axis=0)
    both = lax.dot_general(all_a, full_a, dims, preferred_element_type=jnp.float32)
    both = both + lax.dot_general(
        all_b[:, : width - cut], full_b, dims, preferred_element_type=jnp.float32
    )
    both = both.reshape(count, NX, 2, units)
    expert = lax.axis_index("exp") // NC
    tables = all_b[:, width - cut : width - cut + 2 * experts].astype(jnp.float32)
    pick = (jnp.arange(2 * experts, dtype=jnp.int32) % experts == expert).astype(jnp.float32)
    scale = jnp.sum(tables * pick[None, :], axis=1)
    acts = (jax.nn.silu(both[:, :, 0]) * both[:, :, 1] * scale[:, None, None]).astype(jnp.bfloat16)
    acts = acts.reshape(count, NX * units)
    mine, other = acts[: count // 2], acts[count // 2 :]
    acts = jnp.concatenate([mine, shift(other, c=1)], axis=1)

    down = down_weight[0]
    down_a, down_b = gather_x(down[:, :cut], down[:, cut:])
    down_a = jnp.concatenate(down_a + [shift(v, c=1) for v in down_a], axis=0)
    down_b = jnp.concatenate(down_b + [shift(v, c=1) for v in down_b], axis=0)

    out_a = jnp.dot(acts, down_a, preferred_element_type=jnp.float32).astype(jnp.bfloat16)
    group = count // 2 // NY
    out_a = scatter_y([out_a[d * group : (d + 1) * group] for d in range(NY)])
    out_a = scatter_z([out_a[d * rows : (d + 1) * rows] for d in range(NZ)])

    acts_b = acts.reshape(NY, NZ, rows, -1).transpose(1, 0, 2, 3).reshape(count // 2, -1)
    out_b = jnp.dot(acts_b, down_b, preferred_element_type=jnp.float32).astype(jnp.bfloat16)
    group = count // 2 // NZ
    out_b = scatter_z([out_b[d * group : (d + 1) * group] for d in range(NZ)])
    out_b = scatter_y([out_b[d * rows : (d + 1) * rows] for d in range(NY)])
    moe_out = jnp.concatenate([out_a, out_b], axis=1)

    attn_latent = attend(query_latent, query_rope, cache_latent, cache_rope, lengths)
    return (moe_out, attn_latent)


def solution(mesh):
    return jax.shard_map(
        on_device,
        mesh=mesh,
        in_specs=(
            P(("rep", "exp"), None),
            P(("rep", "exp"), None),
            P(),
            P("exp", "rep", None, None),
            P("exp", "rep", None),
            P(("rep", "exp"), None, None),
            P(("rep", "exp"), None, None),
            P(("rep", "exp"), None, None),
            P(("rep", "exp"), None, None),
            P(("rep", "exp")),
        ),
        out_specs=(P(("rep", "exp"), None), P(("rep", "exp"), None, None)),
        check_vma=False,
    )
```

```python
import functools
import math

import jax
import jax.numpy as jnp
from jax import lax
from jax.experimental import pallas as pl
from jax.experimental.pallas import tpu as pltpu
from jax.sharding import Mesh
from jax.sharding import PartitionSpec as P

ROPE = 64
NOPE = 128
ROUTE_SCALE = 2.827
AXES = ("zl", "x", "y", "zh", "c")
SIZES = (2, 4, 4, 4, 2)
ROWS_OF = ("y", "zh", "zl", "c")
NX, NY, NZ, NC = 4, 4, 8, 2
N_EXPERTS = 16


def index_of(x, y, z, c):
    return (((z % 2) * NX + x) * NY + y) * (NZ // 2) * NC + (z // 2) * NC + c


def shift(value, x=0, y=0, z=0, c=0):
    pairs = []
    for i in range(NX):
        for j in range(NY):
            for k in range(NZ):
                for m in range(NC):
                    pairs.append(
                        (
                            index_of(i, j, k, m),
                            index_of((i + x) % NX, (j + y) % NY, (k + z) % NZ, (m + c) % NC),
                        )
                    )
    return lax.ppermute(value, AXES, pairs)


def exchange_sum(blocks, axis):
    got = lax.all_to_all(blocks, axis, split_axis=0, concat_axis=0, tiled=True)
    return jnp.sum(got.astype(jnp.float32), axis=0).astype(jnp.bfloat16)


def attend(query_latent, query_rope, cache_latent, cache_rope, row_lengths):
    score_scale = 1.0 / math.sqrt(NOPE + ROPE)
    scores = jnp.einsum(
        "rhc,rlc->rhl", query_latent, cache_latent, preferred_element_type=jnp.float32
    )
    scores = scores + jnp.einsum(
        "rhp,rpl->rhl", query_rope, cache_rope, preferred_element_type=jnp.float32
    )
    scores = scores * score_scale
    valid_mask = (
        jnp.arange(cache_latent.shape[1], dtype=jnp.int32)[None, None, :]
        < row_lengths[:, None, None]
    )
    scores = jnp.where(valid_mask, scores, -1e30)
    row_max = jnp.max(scores, axis=2, keepdims=True)
    weights_raw = jnp.where(valid_mask, jnp.exp(scores - row_max), 0.0)
    attn_probs = (weights_raw / jnp.sum(weights_raw, axis=2, keepdims=True)).astype(jnp.bfloat16)
    output = jnp.einsum(
        "rhl,rlc->rhc", attn_probs, cache_latent, preferred_element_type=jnp.float32
    )
    return output.astype(jnp.bfloat16)


def mixing_table(hidden, expert_ids, router):
    logits = jnp.dot(hidden, router, preferred_element_type=jnp.float32)
    experts = router.shape[1]
    named = jnp.any(
        expert_ids[:, :, None] == jnp.arange(experts, dtype=jnp.int32)[None, None, :], axis=1
    )
    gates = jnp.where(named, jax.nn.sigmoid(logits), 0.0)
    return gates / jnp.sum(gates, axis=1, keepdims=True) * ROUTE_SCALE


def hidden_kernel(expert_ref, x_ref, *refs):
    pieces, (out_ref, weights, sems) = refs[:-3], refs[-3:]
    gates, width = weights.shape[0] // 2, weights.shape[1]
    units = gates // NX
    experts = N_EXPERTS

    @pl.when(pl.program_id(0) == 0)
    def _():
        copies = []
        for kind in range(2):
            for shard in range(NX):
                piece = kind * NX + shard
                target = weights.at[pl.ds(piece * units, units), :]
                copies.append(pltpu.make_async_copy(pieces[piece], target, sems.at[piece]))
        for copy in copies:
            copy.start()
        for copy in copies:
            copy.wait()

    both = lax.dot_general(
        x_ref[:, :width],
        weights[...],
        (((1,), (1,)), ((), ())),
        preferred_element_type=jnp.float32,
    )
    table = x_ref[:, width:].astype(jnp.float32)
    lane = lax.broadcasted_iota(jnp.int32, table.shape, 1)
    picked = ((lane & (experts - 1)) == expert_ref[0]) & (lane < 2 * experts)
    scale = jnp.sum(jnp.where(picked, table, 0.0), axis=1, keepdims=True)
    gate, up = both[:, :gates], both[:, gates:]
    acts = (gate / (1.0 + jnp.exp(-gate)) * up * scale).astype(jnp.bfloat16)
    blocks = acts.shape[0] // 32
    acts = acts.reshape(blocks, 2, 16, gates)
    for c in range(NC):
        out_ref[c] = acts[:, c].reshape(blocks * 16, gates)


def hidden_units(everyone, pieces, expert):
    count, wide = everyone.shape
    gates, width = NX * pieces[-1].shape[0], pieces[-1].shape[1]
    block = 256
    return pl.pallas_call(
        hidden_kernel,
        out_shape=jax.ShapeDtypeStruct((NC, count // NC, gates), jnp.bfloat16),
        grid_spec=pltpu.PrefetchScalarGridSpec(
            num_scalar_prefetch=1,
            grid=(count // block,),
            in_specs=[pl.BlockSpec((block, wide), lambda i, e: (i, 0))]
            + [pl.BlockSpec(memory_space=pltpu.HBM)] * len(pieces),
            out_specs=pl.BlockSpec((NC, block // NC, gates), lambda i, e: (0, i, 0)),
            scratch_shapes=[
                pltpu.VMEM((2 * gates, width), jnp.bfloat16),
                pltpu.SemaphoreType.DMA((2 * NX,)),
            ],
        ),
        compiler_params=pltpu.CompilerParams(vmem_limit_bytes=44 << 20),
        cost_estimate=pl.CostEstimate(
            flops=4 * count * gates * width,
            bytes_accessed=2 * (count * wide + 2 * gates * width),
            transcendentals=count * gates,
        ),
        name="hidden_units",
    )(jnp.reshape(expert, (1,)).astype(jnp.int32), everyone, *pieces)


def down_kernel(turn, place_ref, mine_ref, recv_ref, own_ref, twin_ref, out_ref, acts):
    gates = own_ref.shape[0]

    @pl.when(pl.program_id(0) == 0)
    def _():
        if not turn:
            acts[:, :gates] = mine_ref[0]
            acts[:, gates:] = recv_ref[...]
        else:
            rows = mine_ref.shape[1] // (NY * NZ)
            for z in range(NZ):
                for y in range(NY):
                    source = pl.ds((y * NZ + z) * rows, rows)
                    target = pl.ds((z * NY + y) * rows, rows)
                    acts[target, :gates] = mine_ref[0, source, :]
                    acts[target, gates:] = recv_ref[source, :]

    out = jnp.dot(acts[:, :gates], own_ref[...], preferred_element_type=jnp.float32)
    out = out + jnp.dot(acts[:, gates:], twin_ref[...], preferred_element_type=jnp.float32)
    out_ref[...] = out.astype(jnp.bfloat16)


def project(acts, recv, own, twin, place, first, span, turn):
    _, count, gates = acts.shape
    block = 512
    skip = first // block
    return pl.pallas_call(
        functools.partial(down_kernel, turn),
        out_shape=jax.ShapeDtypeStruct((count, span), jnp.bfloat16),
        grid_spec=pltpu.PrefetchScalarGridSpec(
            num_scalar_prefetch=1,
            grid=(span // block,),
            in_specs=[
                pl.BlockSpec((1, count, gates), lambda i, p: (p[0], 0, 0)),
                pl.BlockSpec((count, gates), lambda i, p: (0, 0)),
                pl.BlockSpec((gates, block), lambda i, p: (0, i + skip)),
                pl.BlockSpec((gates, block), lambda i, p: (0, i + skip)),
            ],
            out_specs=pl.BlockSpec((count, block), lambda i, p: (0, i)),
            scratch_shapes=[pltpu.VMEM((count, 2 * gates), jnp.bfloat16)],
        ),
        compiler_params=pltpu.CompilerParams(vmem_limit_bytes=(56 if turn else 16) << 20),
        cost_estimate=pl.CostEstimate(
            flops=4 * count * gates * span,
            bytes_accessed=2 * (2 * gates * span + count * span + 2 * count * gates),
            transcendentals=0,
        ),
        name="project",
    )(place, acts, recv, own, twin)


def on_device(
    hidden,
    expert_ids,
    router,
    gate_up,
    down_weight,
    query_latent,
    query_rope,
    cache_latent,
    cache_rope,
    lengths,
):
    rows, width = hidden.shape
    units = gate_up.shape[1]
    experts = router.shape[1]
    cut = width // 7 * 3
    core = lax.axis_index("c")
    place = jnp.reshape(core, (1,)).astype(jnp.int32)
    expert = lax.axis_index("y") * (NZ // 2) + lax.axis_index("zh")

    mixing = mixing_table(hidden, expert_ids, router)
    high = lax.reduce_precision(mixing, 8, 7)
    low = mixing - high
    table = jnp.concatenate([high, low], axis=1).astype(jnp.bfloat16)
    table = jnp.pad(table, ((0, 0), (0, 128 - 2 * experts)))
    everyone = lax.all_gather(
        jnp.concatenate([hidden, table], axis=1), ROWS_OF, axis=0, tiled=True
    )
    count = everyone.shape[0]

    attn_latent = attend(query_latent, query_rope, cache_latent, cache_rope, lengths)

    own = gate_up[0].transpose(1, 0, 2)
    gate, up = own[0], own[1]
    gate_left, up_left = shift(gate, x=1), shift(up, x=1)
    gate_right, up_right = shift(gate, x=-1), shift(up, x=-1)
    gate_far, up_far = shift(gate_left, x=1), shift(up_right, x=-1)

    down = down_weight[0]
    down_left, down_right = shift(down, x=1), shift(down, x=-1)
    half = units // 2
    far = [shift(down_left[:half], x=1), shift(down_right[half:], x=-1)]
    down = jnp.concatenate([down, down_left, down_right] + far, axis=0)
    twin = shift(down, c=1)

    pieces = [gate, gate_left, gate_right, gate_far, up, up_left, up_right, up_far]
    acts = hidden_units(everyone, pieces, expert)
    recv = shift(lax.dynamic_index_in_dim(acts, 1 - core, axis=0, keepdims=False), c=1)

    out_b = project(acts, recv, down, twin, place, cut, width - cut, True)
    out_b = lax.psum_scatter(out_b, ("zh", "zl"), scatter_dimension=0, tiled=True)
    out_a = project(acts, recv, down, twin, place, 0, cut, False)
    out_a = exchange_sum(out_a.reshape(NY, NZ * rows, cut), "y")
    out_a, out_b = lax.optimization_barrier((out_a, out_b))
    out_a = exchange_sum(out_a.reshape(NZ, rows, cut), ("zh", "zl"))
    out_b = exchange_sum(out_b.reshape(NY, rows, width - cut), "y")
    moe_out = jnp.concatenate([out_a, out_b], axis=1)

    return (moe_out, attn_latent)


def solution(mesh):
    parts = Mesh(mesh.devices.reshape(SIZES), AXES)
    rep, exp = ("zl", "x"), ("y", "zh", "c")
    return jax.shard_map(
        on_device,
        mesh=parts,
        in_specs=(
            P(AXES, None),
            P(AXES, None),
            P(),
            P(exp, rep, None, None),
            P(exp, rep, None),
            P(AXES, None, None),
            P(AXES, None, None),
            P(AXES, None, None),
            P(AXES, None, None),
            P(AXES),
        ),
        out_specs=(P(AXES, None), P(AXES, None, None)),
        check_vma=False,
    )
```

```python
import functools
import math

import jax
import jax.numpy as jnp
from jax import lax
from jax.experimental import pallas as pl
from jax.experimental.pallas import tpu as pltpu
from jax.sharding import Mesh
from jax.sharding import PartitionSpec as P

ROPE = 64
NOPE = 128
ROUTE_SCALE = 2.827
AXES = ("zl", "x", "y", "zh", "c")
SIZES = (2, 4, 4, 4, 2)
ROWS_OF = ("y", "zh", "zl", "c")
NX, NY, NZ, NC = 4, 4, 8, 2
N_EXPERTS = 16


def index_of(x, y, z, c):
    return (((z % 2) * NX + x) * NY + y) * (NZ // 2) * NC + (z // 2) * NC + c


def shift(value, x=0, y=0, z=0, c=0):
    pairs = []
    for i in range(NX):
        for j in range(NY):
            for k in range(NZ):
                for m in range(NC):
                    pairs.append(
                        (
                            index_of(i, j, k, m),
                            index_of((i + x) % NX, (j + y) % NY, (k + z) % NZ, (m + c) % NC),
                        )
                    )
    return lax.ppermute(value, AXES, pairs)


def scatter_y(blocks):
    total = blocks[0].astype(jnp.float32)
    for d in range(1, NY):
        total = total + shift(blocks[d], y=d).astype(jnp.float32)
    return total.astype(jnp.bfloat16)


def exchange_sum(blocks, axis):
    got = lax.all_to_all(blocks, axis, split_axis=0, concat_axis=0, tiled=True)
    return jnp.sum(got.astype(jnp.float32), axis=0).astype(jnp.bfloat16)


def attend(query_latent, query_rope, cache_latent, cache_rope, row_lengths):
    score_scale = 1.0 / math.sqrt(NOPE + ROPE)
    scores = jnp.einsum(
        "rhc,rlc->rhl", query_latent, cache_latent, preferred_element_type=jnp.float32
    )
    scores = scores + jnp.einsum(
        "rhp,rpl->rhl", query_rope, cache_rope, preferred_element_type=jnp.float32
    )
    scores = scores * score_scale
    valid_mask = (
        jnp.arange(cache_latent.shape[1], dtype=jnp.int32)[None, None, :]
        < row_lengths[:, None, None]
    )
    scores = jnp.where(valid_mask, scores, -1e30)
    row_max = jnp.max(scores, axis=2, keepdims=True)
    weights_raw = jnp.where(valid_mask, jnp.exp(scores - row_max), 0.0)
    attn_probs = (weights_raw / jnp.sum(weights_raw, axis=2, keepdims=True)).astype(jnp.bfloat16)
    output = jnp.einsum(
        "rhl,rlc->rhc", attn_probs, cache_latent, preferred_element_type=jnp.float32
    )
    return output.astype(jnp.bfloat16)


def mixing_table(hidden, expert_ids, router):
    logits = jnp.dot(hidden, router, preferred_element_type=jnp.float32)
    experts = router.shape[1]
    named = jnp.any(
        expert_ids[:, :, None] == jnp.arange(experts, dtype=jnp.int32)[None, None, :], axis=1
    )
    gates = jnp.where(named, jax.nn.sigmoid(logits), 0.0)
    return gates / jnp.sum(gates, axis=1, keepdims=True) * ROUTE_SCALE


def hidden_kernel(expert_ref, x_ref, *refs):
    pieces, (out_ref, weights, sems) = refs[:-3], refs[-3:]
    gates, width = weights.shape[0] // 2, weights.shape[1]
    units = gates // NX
    experts = N_EXPERTS

    @pl.when(pl.program_id(0) == 0)
    def _():
        copies = []
        for kind in range(2):
            for shard in range(NX):
                piece = kind * NX + shard
                target = weights.at[pl.ds(piece * units, units), :]
                copies.append(pltpu.make_async_copy(pieces[piece], target, sems.at[piece]))
        for copy in copies:
            copy.start()
        for copy in copies:
            copy.wait()

    both = lax.dot_general(
        x_ref[:, :width],
        weights[...],
        (((1,), (1,)), ((), ())),
        preferred_element_type=jnp.float32,
    )
    table = x_ref[:, width:].astype(jnp.float32)
    lane = lax.broadcasted_iota(jnp.int32, table.shape, 1)
    picked = ((lane & (experts - 1)) == expert_ref[0]) & (lane < 2 * experts)
    scale = jnp.sum(jnp.where(picked, table, 0.0), axis=1, keepdims=True)
    gate, up = both[:, :gates], both[:, gates:]
    acts = (gate / (1.0 + jnp.exp(-gate)) * up * scale).astype(jnp.bfloat16)
    blocks = acts.shape[0] // 32
    acts = acts.reshape(blocks, 2, 16, gates)
    for c in range(NC):
        out_ref[c] = acts[:, c].reshape(blocks * 16, gates)


def hidden_units(everyone, pieces, expert):
    count, wide = everyone.shape
    gates, width = NX * pieces[-1].shape[0], pieces[-1].shape[1]
    block = 256
    return pl.pallas_call(
        hidden_kernel,
        out_shape=jax.ShapeDtypeStruct((NC, count // NC, gates), jnp.bfloat16),
        grid_spec=pltpu.PrefetchScalarGridSpec(
            num_scalar_prefetch=1,
            grid=(count // block,),
            in_specs=[pl.BlockSpec((block, wide), lambda i, e: (i, 0))]
            + [pl.BlockSpec(memory_space=pltpu.HBM)] * len(pieces),
            out_specs=pl.BlockSpec((NC, block // NC, gates), lambda i, e: (0, i, 0)),
            scratch_shapes=[
                pltpu.VMEM((2 * gates, width), jnp.bfloat16),
                pltpu.SemaphoreType.DMA((2 * NX,)),
            ],
        ),
        compiler_params=pltpu.CompilerParams(vmem_limit_bytes=44 << 20),
        cost_estimate=pl.CostEstimate(
            flops=4 * count * gates * width,
            bytes_accessed=2 * (count * wide + 2 * gates * width),
            transcendentals=count * gates,
        ),
        name="hidden_units",
    )(jnp.reshape(expert, (1,)).astype(jnp.int32), everyone, *pieces)


def down_kernel(turn, place_ref, mine_ref, recv_ref, own_ref, twin_ref, *refs):
    outs, acts = refs[:-1], refs[-1]
    gates = own_ref.shape[0]
    count = mine_ref.shape[1]
    rows = count // (NY * NZ)

    @pl.when(pl.program_id(0) == 0)
    def _():
        if turn:
            pairs = [
                (pl.ds((y * NZ + z) * rows, rows), pl.ds((z * NY + y) * rows, rows))
                for z in range(NZ)
                for y in range(NY)
            ]
        else:
            group = count // NY
            pairs = []
            for d in range(NY):
                first = lax.rem(place_ref[1] + d, NY) * group
                pairs.append((pl.ds(pl.multiple_of(first, group), group), pl.ds(d * group, group)))
        for source, target in pairs:
            acts[target, :gates] = mine_ref[0, source, :]
            acts[target, gates:] = recv_ref[source, :]

    out = jnp.dot(acts[:, :gates], own_ref[...], preferred_element_type=jnp.float32)
    out = out + jnp.dot(acts[:, gates:], twin_ref[...], preferred_element_type=jnp.float32)
    out = out.astype(jnp.bfloat16)
    part = count // len(outs)
    for i, out_ref in enumerate(outs):
        out_ref[...] = out[i * part : (i + 1) * part]


def project(acts, recv, own, twin, place, first, span, turn):
    _, count, gates = acts.shape
    block = 512
    skip = first // block
    number = 1 if turn else NY
    return pl.pallas_call(
        functools.partial(down_kernel, turn),
        out_shape=[jax.ShapeDtypeStruct((count // number, span), jnp.bfloat16)] * number,
        grid_spec=pltpu.PrefetchScalarGridSpec(
            num_scalar_prefetch=1,
            grid=(span // block,),
            in_specs=[
                pl.BlockSpec((1, count, gates), lambda i, p: (p[0], 0, 0)),
                pl.BlockSpec((count, gates), lambda i, p: (0, 0)),
                pl.BlockSpec((gates, block), lambda i, p: (0, i + skip)),
                pl.BlockSpec((gates, block), lambda i, p: (0, i + skip)),
            ],
            out_specs=[pl.BlockSpec((count // number, block), lambda i, p: (0, i))] * number,
            scratch_shapes=[pltpu.VMEM((count, 2 * gates), jnp.bfloat16)],
        ),
        compiler_params=pltpu.CompilerParams(vmem_limit_bytes=50 << 20),
        cost_estimate=pl.CostEstimate(
            flops=4 * count * gates * span,
            bytes_accessed=2 * (2 * gates * span + count * span + 2 * count * gates),
            transcendentals=0,
        ),
        name="project",
    )(place, acts, recv, own, twin)


def on_device(
    hidden,
    expert_ids,
    router,
    gate_up,
    down_weight,
    query_latent,
    query_rope,
    cache_latent,
    cache_rope,
    lengths,
):
    rows, width = hidden.shape
    units = gate_up.shape[1]
    experts = router.shape[1]
    cut = width // 7 * 3
    core = lax.axis_index("c")
    place_y = lax.axis_index("y")
    place = jnp.stack([core, place_y]).astype(jnp.int32)
    expert = lax.axis_index("y") * (NZ // 2) + lax.axis_index("zh")

    mixing = mixing_table(hidden, expert_ids, router)
    high = lax.reduce_precision(mixing, 8, 7)
    low = mixing - high
    table = jnp.concatenate([high, low], axis=1).astype(jnp.bfloat16)
    table = jnp.pad(table, ((0, 0), (0, 128 - 2 * experts)))
    everyone = lax.all_gather(
        jnp.concatenate([hidden, table], axis=1), ROWS_OF, axis=0, tiled=True
    )
    count = everyone.shape[0]

    attn_latent = attend(query_latent, query_rope, cache_latent, cache_rope, lengths)

    own = gate_up[0].transpose(1, 0, 2)
    gate, up = own[0], own[1]
    gate_left, up_left = shift(gate, x=1), shift(up, x=1)
    gate_right, up_right = shift(gate, x=-1), shift(up, x=-1)
    gate_far, up_far = shift(gate_left, x=1), shift(up_right, x=-1)

    down = down_weight[0]
    down_left, down_right = shift(down, x=1), shift(down, x=-1)
    half = units // 2
    far = [shift(down_left[:half], x=1), shift(down_right[half:], x=-1)]
    down = jnp.concatenate([down, down_left, down_right] + far, axis=0)
    twin = shift(down, c=1)

    pieces = [gate, gate_left, gate_right, gate_far, up, up_left, up_right, up_far]
    acts = hidden_units(everyone, pieces, expert)
    recv = shift(lax.dynamic_index_in_dim(acts, 1 - core, axis=0, keepdims=False), c=1)

    (out_b,) = project(acts, recv, down, twin, place, cut, width - cut, True)
    out_b = lax.psum_scatter(out_b, ("zh", "zl"), scatter_dimension=0, tiled=True)
    out_a = project(acts, recv, down, twin, place, 0, cut, False)
    out_a = scatter_y(out_a)
    out_a = exchange_sum(out_a.reshape(NZ, rows, cut), ("zh", "zl"))
    out_b = out_b.reshape(NY, rows, width - cut)
    out_b = scatter_y(
        [lax.dynamic_index_in_dim(out_b, (place_y + d) % NY, keepdims=False) for d in range(NY)]
    )
    moe_out = jnp.concatenate([out_a, out_b], axis=1)

    return (moe_out, attn_latent)


def solution(mesh):
    parts = Mesh(mesh.devices.reshape(SIZES), AXES)
    rep, exp = ("zl", "x"), ("y", "zh", "c")
    return jax.shard_map(
        on_device,
        mesh=parts,
        in_specs=(
            P(AXES, None),
            P(AXES, None),
            P(),
            P(exp, rep, None, None),
            P(exp, rep, None),
            P(AXES, None, None),
            P(AXES, None, None),
            P(AXES, None, None),
            P(AXES, None, None),
            P(AXES),
        ),
        out_specs=(P(AXES, None), P(AXES, None, None)),
        check_vma=False,
    )
```

```python
import functools
import math

import jax
import jax.numpy as jnp
from jax import lax
from jax.experimental import pallas as pl
from jax.experimental.pallas import tpu as pltpu
from jax.sharding import Mesh
from jax.sharding import PartitionSpec as P

ROPE = 64
NOPE = 128
ROUTE_SCALE = 2.827
AXES = ("zl", "x", "y", "zh", "c")
SIZES = (2, 4, 4, 4, 2)
ROWS_OF = ("y", "zh", "zl", "c")
NX, NY, NZ, NC = 4, 4, 8, 2
N_EXPERTS = 16


def index_of(x, y, z, c):
    return (((z % 2) * NX + x) * NY + y) * (NZ // 2) * NC + (z // 2) * NC + c


def shift(value, x=0, y=0, z=0, c=0):
    pairs = []
    for i in range(NX):
        for j in range(NY):
            for k in range(NZ):
                for m in range(NC):
                    pairs.append(
                        (
                            index_of(i, j, k, m),
                            index_of((i + x) % NX, (j + y) % NY, (k + z) % NZ, (m + c) % NC),
                        )
                    )
    return lax.ppermute(value, AXES, pairs)


def marker(value):
    return jnp.isnan(value[0, 0]).astype(jnp.int32)


def scatter_y(blocks):
    total = blocks[0].astype(jnp.float32)
    for d in range(1, NY):
        total = total + shift(blocks[d], y=d).astype(jnp.float32)
    return total.astype(jnp.bfloat16)


def add(*values):
    return sum(v.astype(jnp.float32) for v in values).astype(jnp.bfloat16)


def scatter_ring_y(blocks):
    half = blocks[0].shape[1] // 2
    up, down = shift(blocks[2][:, :half], y=1), shift(blocks[2][:, half:], y=-1)
    up = jnp.concatenate([add(up, blocks[1][:, :half]), blocks[1][:, half:]], axis=1)
    down = jnp.concatenate([blocks[3][:, :half], add(down, blocks[3][:, half:])], axis=1)
    return add(blocks[0], shift(up, y=1), shift(down, y=-1))


def exchange_sum(blocks, axis):
    got = lax.all_to_all(blocks, axis, split_axis=0, concat_axis=0, tiled=True)
    return jnp.sum(got.astype(jnp.float32), axis=0).astype(jnp.bfloat16)


def attend(query_latent, query_rope, cache_latent, cache_rope, row_lengths):
    score_scale = 1.0 / math.sqrt(NOPE + ROPE)
    scores = jnp.einsum(
        "rhc,rlc->rhl", query_latent, cache_latent, preferred_element_type=jnp.float32
    )
    scores = scores + jnp.einsum(
        "rhp,rpl->rhl", query_rope, cache_rope, preferred_element_type=jnp.float32
    )
    scores = scores * score_scale
    valid_mask = (
        jnp.arange(cache_latent.shape[1], dtype=jnp.int32)[None, None, :]
        < row_lengths[:, None, None]
    )
    scores = jnp.where(valid_mask, scores, -1e30)
    row_max = jnp.max(scores, axis=2, keepdims=True)
    weights_raw = jnp.where(valid_mask, jnp.exp(scores - row_max), 0.0)
    attn_probs = (weights_raw / jnp.sum(weights_raw, axis=2, keepdims=True)).astype(jnp.bfloat16)
    output = jnp.einsum(
        "rhl,rlc->rhc", attn_probs, cache_latent, preferred_element_type=jnp.float32
    )
    return output.astype(jnp.bfloat16)


def mixing_table(hidden, expert_ids, router):
    logits = jnp.dot(hidden, router, preferred_element_type=jnp.float32)
    experts = router.shape[1]
    named = jnp.any(
        expert_ids[:, :, None] == jnp.arange(experts, dtype=jnp.int32)[None, None, :], axis=1
    )
    gates = jnp.where(named, jax.nn.sigmoid(logits), 0.0)
    return gates / jnp.sum(gates, axis=1, keepdims=True) * ROUTE_SCALE


def hidden_kernel(expert_ref, x_ref, *refs):
    pieces, (out_ref, weights, sems) = refs[:-3], refs[-3:]
    gates, width = weights.shape[0] // 2, weights.shape[1]
    units = gates // NX
    experts = N_EXPERTS

    @pl.when(pl.program_id(0) == 0)
    def _():
        copies = []
        for kind in range(2):
            for shard in range(NX):
                piece = kind * NX + shard
                target = weights.at[pl.ds(piece * units, units), :]
                copies.append(pltpu.make_async_copy(pieces[piece], target, sems.at[piece]))
        for copy in copies:
            copy.start()
        for copy in copies:
            copy.wait()

    both = lax.dot_general(
        x_ref[:, :width],
        weights[...],
        (((1,), (1,)), ((), ())),
        preferred_element_type=jnp.float32,
    )
    table = x_ref[:, width:].astype(jnp.float32)
    lane = lax.broadcasted_iota(jnp.int32, table.shape, 1)
    picked = ((lane & (experts - 1)) == expert_ref[0]) & (lane < 2 * experts)
    scale = jnp.sum(jnp.where(picked, table, 0.0), axis=1, keepdims=True)
    gate, up = both[:, :gates], both[:, gates:]
    acts = (gate / (1.0 + jnp.exp(-gate)) * up * scale).astype(jnp.bfloat16)
    blocks = acts.shape[0] // 32
    acts = acts.reshape(blocks, 2, 16, gates)
    for c in range(NC):
        out_ref[c] = acts[:, c].reshape(blocks * 16, gates)


def hidden_units(everyone, pieces, expert):
    count, wide = everyone.shape
    gates, width = NX * pieces[-1].shape[0], pieces[-1].shape[1]
    block = 256
    return pl.pallas_call(
        hidden_kernel,
        out_shape=jax.ShapeDtypeStruct((NC, count // NC, gates), jnp.bfloat16),
        grid_spec=pltpu.PrefetchScalarGridSpec(
            num_scalar_prefetch=1,
            grid=(count // block,),
            in_specs=[pl.BlockSpec((block, wide), lambda i, e: (i, 0))]
            + [pl.BlockSpec(memory_space=pltpu.HBM)] * len(pieces),
            out_specs=pl.BlockSpec((NC, block // NC, gates), lambda i, e: (0, i, 0)),
            scratch_shapes=[
                pltpu.VMEM((2 * gates, width), jnp.bfloat16),
                pltpu.SemaphoreType.DMA((2 * NX,)),
            ],
        ),
        compiler_params=pltpu.CompilerParams(vmem_limit_bytes=44 << 20),
        cost_estimate=pl.CostEstimate(
            flops=4 * count * gates * width,
            bytes_accessed=2 * (count * wide + 2 * gates * width),
            transcendentals=count * gates,
        ),
        name="hidden_units",
    )(jnp.reshape(expert, (1,)).astype(jnp.int32), everyone, *pieces)


def down_kernel(turn, place_ref, mine_ref, recv_ref, own_ref, twin_ref, *refs):
    outs, acts = refs[:-1], refs[-1]
    gates = own_ref.shape[0]
    count = mine_ref.shape[1]
    rows = count // (NY * NZ)

    @pl.when(pl.program_id(0) == 0)
    def _():
        if turn:
            pairs = [
                (pl.ds((y * NZ + z) * rows, rows), pl.ds((z * NY + y) * rows, rows))
                for z in range(NZ)
                for y in range(NY)
            ]
        else:
            group = count // NY
            pairs = []
            for d in range(NY):
                first = lax.rem(place_ref[1] + d, NY) * group
                pairs.append((pl.ds(pl.multiple_of(first, group), group), pl.ds(d * group, group)))
        for source, target in pairs:
            acts[target, :gates] = mine_ref[0, source, :]
            acts[target, gates:] = recv_ref[source, :]

    out = jnp.dot(acts[:, :gates], own_ref[...], preferred_element_type=jnp.float32)
    out = out + jnp.dot(acts[:, gates:], twin_ref[...], preferred_element_type=jnp.float32)
    out = out.astype(jnp.bfloat16)
    part = count // len(outs)
    for i, out_ref in enumerate(outs):
        out_ref[...] = out[i * part : (i + 1) * part]


def project(acts, recv, own, twin, place, first, span, block, turn):
    _, count, gates = acts.shape
    window = pl.BlockSpec(
        (pl.Element(gates), pl.Element(block)), lambda i, p: (0, pl.multiple_of(first + i * block, 128))
    )
    number = 1 if turn else NY
    return pl.pallas_call(
        functools.partial(down_kernel, turn),
        out_shape=[jax.ShapeDtypeStruct((count // number, span), jnp.bfloat16)] * number,
        grid_spec=pltpu.PrefetchScalarGridSpec(
            num_scalar_prefetch=1,
            grid=(span // block,),
            in_specs=[
                pl.BlockSpec((1, count, gates), lambda i, p: (p[0], 0, 0)),
                pl.BlockSpec((count, gates), lambda i, p: (0, 0)),
                window,
                window,
            ],
            out_specs=[pl.BlockSpec((count // number, block), lambda i, p: (0, i))] * number,
            scratch_shapes=[pltpu.VMEM((count, 2 * gates), jnp.bfloat16)],
        ),
        compiler_params=pltpu.CompilerParams(vmem_limit_bytes=50 << 20),
        cost_estimate=pl.CostEstimate(
            flops=4 * count * gates * span,
            bytes_accessed=2 * (2 * gates * span + count * span + 2 * count * gates),
            transcendentals=0,
        ),
        name="project",
    )(place, acts, recv, own, twin)


def on_device(
    hidden,
    expert_ids,
    router,
    gate_up,
    down_weight,
    query_latent,
    query_rope,
    cache_latent,
    cache_rope,
    lengths,
):
    rows, width = hidden.shape
    units = gate_up.shape[1]
    experts = router.shape[1]
    core = lax.axis_index("c")
    place_y = lax.axis_index("y")
    place = jnp.stack([core, place_y]).astype(jnp.int32)
    expert = lax.axis_index("y") * (NZ // 2) + lax.axis_index("zh")

    mixing = mixing_table(hidden, expert_ids, router)
    high = lax.reduce_precision(mixing, 8, 7)
    low = mixing - high
    table = jnp.concatenate([high, low], axis=1).astype(jnp.bfloat16)
    table = jnp.pad(table, ((0, 0), (0, 128 - 2 * experts)))
    everyone = lax.all_gather(
        jnp.concatenate([hidden, table], axis=1), ROWS_OF, axis=0, tiled=True
    )
    count = everyone.shape[0]


    own = gate_up[0].transpose(1, 0, 2)
    gate, up = own[0], own[1]
    gate_left, up_left = shift(gate, x=1), shift(up, x=1)
    gate_right, up_right = shift(gate, x=-1), shift(up, x=-1)
    gate_far, up_far = shift(gate_left, x=1), shift(up_right, x=-1)

    attn_latent = attend(query_latent, query_rope, cache_latent, cache_rope, lengths)
    ready = marker(attn_latent[0])
    down = down_weight[0]
    down_left, down_right = shift(down, x=1), shift(down, x=-1)
    half = units // 2
    far = [
        shift(lax.dynamic_slice_in_dim(down_left, ready, half, axis=0), x=1),
        shift(lax.dynamic_slice_in_dim(down_right, half + ready, half, axis=0), x=-1),
    ]
    down = jnp.concatenate([down, down_left, down_right] + far, axis=0)
    twin = shift(down, c=1)

    pieces = [gate, gate_left, gate_right, gate_far, up, up_left, up_right, up_far]
    acts = hidden_units(everyone, pieces, expert)
    recv = shift(lax.dynamic_index_in_dim(acts, 1 - core, axis=0, keepdims=False), c=1)

    cut = width // 28 * 13
    inputs = (acts, recv, down, twin, place)
    (out_b,) = project(*inputs, cut, width - cut, (width - cut) // 3, True)
    out_b = lax.psum_scatter(out_b, ("zh", "zl"), scatter_dimension=0, tiled=True)
    out_a = scatter_ring_y(project(*inputs, 0, cut, cut // 2, False))
    out_a = exchange_sum(out_a.reshape(NZ, rows, cut), ("zh", "zl"))
    out_b = out_b.reshape(NY, rows, width - cut)
    out_b = scatter_y(
        [lax.dynamic_index_in_dim(out_b, (place_y + d) % NY, keepdims=False) for d in range(NY)]
    )
    moe_out = jnp.concatenate([out_a, out_b], axis=1)

    return (moe_out, attn_latent)


def solution(mesh):
    parts = Mesh(mesh.devices.reshape(SIZES), AXES)
    rep, exp = ("zl", "x"), ("y", "zh", "c")
    return jax.shard_map(
        on_device,
        mesh=parts,
        in_specs=(
            P(AXES, None),
            P(AXES, None),
            P(),
            P(exp, rep, None, None),
            P(exp, rep, None),
            P(AXES, None, None),
            P(AXES, None, None),
            P(AXES, None, None),
            P(AXES, None, None),
            P(AXES),
        ),
        out_specs=(P(AXES, None), P(AXES, None, None)),
        check_vma=False,
    )
```

```python
import functools
import math

import jax
import jax.numpy as jnp
from jax import lax
from jax.experimental import pallas as pl
from jax.experimental.pallas import tpu as pltpu
from jax.sharding import Mesh
from jax.sharding import PartitionSpec as P

ROPE = 64
NOPE = 128
ROUTE_SCALE = 2.827
AXES = ("zl", "x", "y", "zh", "c")
SIZES = (2, 4, 4, 4, 2)
ROWS_OF = ("y", "zh", "zl", "c")
NX, NY, NZ, NC = 4, 4, 8, 2
N_EXPERTS = 16


def index_of(x, y, z, c):
    return (((z % 2) * NX + x) * NY + y) * (NZ // 2) * NC + (z // 2) * NC + c


def shift(value, x=0, y=0, z=0, c=0):
    pairs = []
    for i in range(NX):
        for j in range(NY):
            for k in range(NZ):
                for m in range(NC):
                    pairs.append(
                        (
                            index_of(i, j, k, m),
                            index_of((i + x) % NX, (j + y) % NY, (k + z) % NZ, (m + c) % NC),
                        )
                    )
    return lax.ppermute(value, AXES, pairs)


def marker(value):
    return jnp.isnan(value[0, 0]).astype(jnp.int32)


def scatter_y(blocks):
    total = blocks[0].astype(jnp.float32)
    for d in range(1, NY):
        total = total + shift(blocks[d], y=d).astype(jnp.float32)
    return total.astype(jnp.bfloat16)


def add(*values):
    return sum(v.astype(jnp.float32) for v in values).astype(jnp.bfloat16)


def scatter_ring_y(blocks):
    half = blocks[0].shape[1] // 2
    up, down = shift(blocks[2][:, :half], y=1), shift(blocks[2][:, half:], y=-1)
    free_up, free_down = shift(blocks[1][:, half:], y=1), shift(blocks[3][:, :half], y=-1)
    up = shift(add(up, blocks[1][:, :half]), y=1)
    down = shift(add(down, blocks[3][:, half:]), y=-1)
    own = blocks[0]
    return jnp.concatenate(
        [add(own[:, :half], up, free_down), add(own[:, half:], free_up, down)], axis=1
    )


def exchange_sum(blocks, axis):
    got = lax.all_to_all(blocks, axis, split_axis=0, concat_axis=0, tiled=True)
    return jnp.sum(got.astype(jnp.float32), axis=0).astype(jnp.bfloat16)


def attend(query_latent, query_rope, cache_latent, cache_rope, row_lengths):
    score_scale = 1.0 / math.sqrt(NOPE + ROPE)
    scores = jnp.einsum(
        "rhc,rlc->rhl", query_latent, cache_latent, preferred_element_type=jnp.float32
    )
    scores = scores + jnp.einsum(
        "rhp,rpl->rhl", query_rope, cache_rope, preferred_element_type=jnp.float32
    )
    scores = scores * score_scale
    valid_mask = (
        jnp.arange(cache_latent.shape[1], dtype=jnp.int32)[None, None, :]
        < row_lengths[:, None, None]
    )
    scores = jnp.where(valid_mask, scores, -1e30)
    row_max = jnp.max(scores, axis=2, keepdims=True)
    weights_raw = jnp.where(valid_mask, jnp.exp(scores - row_max), 0.0)
    attn_probs = (weights_raw / jnp.sum(weights_raw, axis=2, keepdims=True)).astype(jnp.bfloat16)
    output = jnp.einsum(
        "rhl,rlc->rhc", attn_probs, cache_latent, preferred_element_type=jnp.float32
    )
    return output.astype(jnp.bfloat16)


def mixing_table(hidden, expert_ids, router):
    logits = jnp.dot(hidden, router, preferred_element_type=jnp.float32)
    experts = router.shape[1]
    named = jnp.any(
        expert_ids[:, :, None] == jnp.arange(experts, dtype=jnp.int32)[None, None, :], axis=1
    )
    gates = jnp.where(named, jax.nn.sigmoid(logits), 0.0)
    return gates / jnp.sum(gates, axis=1, keepdims=True) * ROUTE_SCALE


def hidden_kernel(expert_ref, x_ref, *refs):
    pieces, (out_ref, weights, sems) = refs[:-3], refs[-3:]
    gates, width = weights.shape[0] // 2, weights.shape[1]
    units = gates // NX
    experts = N_EXPERTS

    @pl.when(pl.program_id(0) == 0)
    def _():
        copies = []
        for kind in range(2):
            for shard in range(NX):
                piece = kind * NX + shard
                target = weights.at[pl.ds(piece * units, units), :]
                copies.append(pltpu.make_async_copy(pieces[piece], target, sems.at[piece]))
        for copy in copies:
            copy.start()
        for copy in copies:
            copy.wait()

    both = lax.dot_general(
        x_ref[:, :width],
        weights[...],
        (((1,), (1,)), ((), ())),
        preferred_element_type=jnp.float32,
    )
    table = x_ref[:, width:].astype(jnp.float32)
    lane = lax.broadcasted_iota(jnp.int32, table.shape, 1)
    picked = ((lane & (experts - 1)) == expert_ref[0]) & (lane < 2 * experts)
    scale = jnp.sum(jnp.where(picked, table, 0.0), axis=1, keepdims=True)
    gate, up = both[:, :gates], both[:, gates:]
    acts = (gate / (1.0 + jnp.exp(-gate)) * up * scale).astype(jnp.bfloat16)
    blocks = acts.shape[0] // 32
    acts = acts.reshape(blocks, 2, 16, gates)
    for c in range(NC):
        out_ref[c] = acts[:, c].reshape(blocks * 16, gates)


def hidden_units(everyone, pieces, expert):
    count, wide = everyone.shape
    gates, width = NX * pieces[-1].shape[0], pieces[-1].shape[1]
    block = 256
    return pl.pallas_call(
        hidden_kernel,
        out_shape=jax.ShapeDtypeStruct((NC, count // NC, gates), jnp.bfloat16),
        grid_spec=pltpu.PrefetchScalarGridSpec(
            num_scalar_prefetch=1,
            grid=(count // block,),
            in_specs=[pl.BlockSpec((block, wide), lambda i, e: (i, 0))]
            + [pl.BlockSpec(memory_space=pltpu.HBM)] * len(pieces),
            out_specs=pl.BlockSpec((NC, block // NC, gates), lambda i, e: (0, i, 0)),
            scratch_shapes=[
                pltpu.VMEM((2 * gates, width), jnp.bfloat16),
                pltpu.SemaphoreType.DMA((2 * NX,)),
            ],
        ),
        compiler_params=pltpu.CompilerParams(vmem_limit_bytes=44 << 20),
        cost_estimate=pl.CostEstimate(
            flops=4 * count * gates * width,
            bytes_accessed=2 * (count * wide + 2 * gates * width),
            transcendentals=count * gates,
        ),
        name="hidden_units",
    )(jnp.reshape(expert, (1,)).astype(jnp.int32), everyone, *pieces)


def down_kernel(turn, place_ref, mine_ref, recv_ref, own_ref, twin_ref, *refs):
    outs, acts = refs[:-1], refs[-1]
    gates = own_ref.shape[0]
    count = mine_ref.shape[1]
    rows = count // (NY * NZ)

    @pl.when(pl.program_id(0) == 0)
    def _():
        if turn:
            pairs = [
                (pl.ds((y * NZ + z) * rows, rows), pl.ds((z * NY + y) * rows, rows))
                for z in range(NZ)
                for y in range(NY)
            ]
        else:
            group = count // NY
            pairs = []
            for d in range(NY):
                first = lax.rem(place_ref[1] + d, NY) * group
                pairs.append((pl.ds(pl.multiple_of(first, group), group), pl.ds(d * group, group)))
        for source, target in pairs:
            acts[target, :gates] = mine_ref[0, source, :]
            acts[target, gates:] = recv_ref[source, :]

    out = jnp.dot(acts[:, :gates], own_ref[...], preferred_element_type=jnp.float32)
    out = out + jnp.dot(acts[:, gates:], twin_ref[...], preferred_element_type=jnp.float32)
    out = out.astype(jnp.bfloat16)
    part = count // len(outs)
    for i, out_ref in enumerate(outs):
        out_ref[...] = out[i * part : (i + 1) * part]


def project(acts, recv, own, twin, place, first, span, block, turn):
    _, count, gates = acts.shape
    window = pl.BlockSpec(
        (pl.Element(gates), pl.Element(block)), lambda i, p: (0, pl.multiple_of(first + i * block, 128))
    )
    number = 1 if turn else NY
    return pl.pallas_call(
        functools.partial(down_kernel, turn),
        out_shape=[jax.ShapeDtypeStruct((count // number, span), jnp.bfloat16)] * number,
        grid_spec=pltpu.PrefetchScalarGridSpec(
            num_scalar_prefetch=1,
            grid=(span // block,),
            in_specs=[
                pl.BlockSpec((1, count, gates), lambda i, p: (p[0], 0, 0)),
                pl.BlockSpec((count, gates), lambda i, p: (0, 0)),
                window,
                window,
            ],
            out_specs=[pl.BlockSpec((count // number, block), lambda i, p: (0, i))] * number,
            scratch_shapes=[pltpu.VMEM((count, 2 * gates), jnp.bfloat16)],
        ),
        compiler_params=pltpu.CompilerParams(vmem_limit_bytes=50 << 20),
        cost_estimate=pl.CostEstimate(
            flops=4 * count * gates * span,
            bytes_accessed=2 * (2 * gates * span + count * span + 2 * count * gates),
            transcendentals=0,
        ),
        name="project",
    )(place, acts, recv, own, twin)


def on_device(
    hidden,
    expert_ids,
    router,
    gate_up,
    down_weight,
    query_latent,
    query_rope,
    cache_latent,
    cache_rope,
    lengths,
):
    rows, width = hidden.shape
    units = gate_up.shape[1]
    experts = router.shape[1]
    core = lax.axis_index("c")
    place_y = lax.axis_index("y")
    place = jnp.stack([core, place_y]).astype(jnp.int32)
    expert = lax.axis_index("y") * (NZ // 2) + lax.axis_index("zh")

    mixing = mixing_table(hidden, expert_ids, router)
    high = lax.reduce_precision(mixing, 8, 7)
    low = mixing - high
    table = jnp.concatenate([high, low], axis=1).astype(jnp.bfloat16)
    table = jnp.pad(table, ((0, 0), (0, 128 - 2 * experts)))
    everyone = lax.all_gather(
        jnp.concatenate([hidden, table], axis=1), ROWS_OF, axis=0, tiled=True
    )
    count = everyone.shape[0]


    own = gate_up[0].transpose(1, 0, 2)
    gate, up = own[0], own[1]
    gate_left, up_left = shift(gate, x=1), shift(up, x=1)
    gate_right, up_right = shift(gate, x=-1), shift(up, x=-1)
    gate_far, up_far = shift(gate_left, x=1), shift(up_right, x=-1)

    attn_latent = attend(query_latent, query_rope, cache_latent, cache_rope, lengths)
    ready = marker(attn_latent[0])
    down = down_weight[0]
    down_left, down_right = shift(down, x=1), shift(down, x=-1)
    half = units // 2
    far = [
        shift(lax.dynamic_slice_in_dim(down_left, ready, half, axis=0), x=1),
        shift(lax.dynamic_slice_in_dim(down_right, half + ready, half, axis=0), x=-1),
    ]
    down = jnp.concatenate([down, down_left, down_right] + far, axis=0)
    twin = shift(down, c=1)

    pieces = [gate, gate_left, gate_right, gate_far, up, up_left, up_right, up_far]
    acts = hidden_units(everyone, pieces, expert)
    recv = shift(lax.dynamic_index_in_dim(acts, 1 - core, axis=0, keepdims=False), c=1)

    cut = width // 28 * 13
    inputs = (acts, recv, down, twin, place)
    (out_b,) = project(*inputs, cut, width - cut, (width - cut) // 3, True)
    out_b = lax.psum_scatter(out_b, ("zh", "zl"), scatter_dimension=0, tiled=True)
    out_a = scatter_ring_y(project(*inputs, 0, cut, cut // 2, False))
    out_a = exchange_sum(out_a.reshape(NZ, rows, cut), ("zh", "zl"))
    out_b = out_b.reshape(NY, rows, width - cut)
    out_b = scatter_y(
        [lax.dynamic_index_in_dim(out_b, (place_y + d) % NY, keepdims=False) for d in range(NY)]
    )
    moe_out = jnp.concatenate([out_a, out_b], axis=1)

    return (moe_out, attn_latent)


def solution(mesh):
    parts = Mesh(mesh.devices.reshape(SIZES), AXES)
    rep, exp = ("zl", "x"), ("y", "zh", "c")
    return jax.shard_map(
        on_device,
        mesh=parts,
        in_specs=(
            P(AXES, None),
            P(AXES, None),
            P(),
            P(exp, rep, None, None),
            P(exp, rep, None),
            P(AXES, None, None),
            P(AXES, None, None),
            P(AXES, None, None),
            P(AXES, None, None),
            P(AXES),
        ),
        out_specs=(P(AXES, None), P(AXES, None, None)),
        check_vma=False,
    )
```
